512 devices in a mesh: gx: 32 (over z, core), gy: 16 (over y, x).
Axes of the slice: x: 4, y: 4, z: 16, core: 2. Of those that a mesh axis runs over, the one named last changes fastest.
Arguments:
- density: float32 [2, 512, 512, 128], P(None, 'gx', 'gy'), may hold values from 0.2 to 1
- cotangent: float32 [2, 512, 512, 128], P(None, 'gx', 'gy'), may hold values from -6 to 6
- adhesion: float32 [2, 2], replicated, may hold values from 1 to 3
Outputs:
- density_bar: float32 [2, 512, 512, 128], P(None, 'gx', 'gy')
The draws below stay inside these ranges and needn't reach their ends.
All inputs are finite; a program needn't handle non-finite values.
Results may differ from the reference program's by a relative error of at most 0.000084.
Values sent between devices are 32-bit elements; how exact they have to be, the bound alone decides.
No kernel may reach another device: no remote copies, remote signals or barrier semaphores. Data moves between devices by JAX's collectives and lax.ppermute only.
A program may use at most 64 MiB of HBM per device.

```python
import jax
import jax.numpy as jnp
from jax import lax

RADIUS = 16
CZ = 128
NX = 512
NY = 512


def draw_density(key, part):
    key_rows, key_cols, key_cells = jax.random.split(jax.random.fold_in(key, 11), 3)
    profile_rows = jax.random.uniform(key_rows, (2, NX, 1, 1), jnp.float32, -1.0, 1.0)
    profile_cols = jax.random.uniform(key_cols, (2, 1, NY, 1), jnp.float32, -1.0, 1.0)
    cells = jax.random.uniform(key_cells, (2, NX, NY, CZ), jnp.float32, -1.0, 1.0)
    result = 0.6 + 0.15 * profile_rows + 0.15 * profile_cols + 0.1 * cells
    return result.astype(jnp.float32)


def draw_cotangent(key, part):
    key_rows, key_cols, key_cells = jax.random.split(jax.random.fold_in(key, 23), 3)
    profile_rows = jax.random.uniform(key_rows, (2, NX, 1, 1), jnp.float32, -1.7, 1.7)
    profile_cols = jax.random.uniform(key_cols, (2, 1, NY, 1), jnp.float32, -1.7, 1.7)
    cells = jnp.clip(jax.random.normal(key_cells, (2, NX, NY, CZ), jnp.float32), -4.5, 4.5)
    result = 0.25 * profile_rows + 0.25 * profile_cols + 0.8 * cells
    return result.astype(jnp.float32)


def setup_inputs(seed: int = 0) -> dict:
    seeds = jax.random.split(jax.random.key(seed), 4)
    density = draw_density(jax.random.fold_in(seeds[3], 71), 0)
    cotangent = draw_cotangent(jax.random.fold_in(seeds[3], 71), 0)
    adhesion = jnp.clip(jax.random.uniform(seeds[2], (2, 2), jnp.float32, 1.0, 3.0), 1.0, 3.0)
    return dict(density=density, cotangent=cotangent, adhesion=adhesion)


time_step = 0.5
smoothing = 0.1

def kernel_taps(antisym):
    offsets = jnp.arange(-RADIUS, RADIUS + 1).astype(jnp.float32)
    weights = 1.0 - jnp.abs(offsets) / (RADIUS + 1.0)
    if antisym:
        weights = weights * offsets / RADIUS
    return weights / jnp.sqrt(jnp.sum(weights * weights))

def correlate(values, taps, along):
    length = values.shape[along]
    widths = [(0, 0)] * values.ndim
    widths[along] = (RADIUS, RADIUS)
    padded = jnp.pad(values, widths)
    result = jnp.zeros_like(values)
    for offset in range(2 * RADIUS + 1):
        result = result + taps[offset] * lax.slice_in_dim(padded, offset, offset + length, axis=along)
    return result

def face_flux(density, velocity, along):
    length = density.shape[along]
    lower_density = lax.slice_in_dim(density, 0, length - 1, axis=along)
    upper_density = lax.slice_in_dim(density, 1, length, axis=along)
    face_velocity = 0.5 * (lax.slice_in_dim(velocity, 0, length - 1, axis=along) + lax.slice_in_dim(velocity, 1, length, axis=along))
    magnitude = jnp.sqrt(face_velocity * face_velocity + smoothing * smoothing)
    flux_value = face_velocity * 0.5 * (lower_density + upper_density) - magnitude * 0.5 * (upper_density - lower_density)
    widths = [(0, 0)] * density.ndim
    widths[along] = (1, 1)
    padded = jnp.pad(flux_value, widths)
    return lax.slice_in_dim(padded, 1, length + 1, axis=along) - lax.slice_in_dim(padded, 0, length, axis=along)

def adhesion_step(density, potential):
    even_taps = kernel_taps(False)
    odd_taps = kernel_taps(True)
    even_in_z = correlate(potential, even_taps, 2)
    odd_in_z = correlate(potential, odd_taps, 2)
    velocity_x = correlate(correlate(even_in_z, even_taps, 1), odd_taps, 0)
    velocity_y = correlate(correlate(even_in_z, odd_taps, 1), even_taps, 0)
    velocity_z = correlate(correlate(odd_in_z, even_taps, 1), even_taps, 0)
    change = face_flux(density, velocity_x, 0) + face_flux(density, velocity_y, 1) + face_flux(density, velocity_z, 2)
    return density - time_step * change

def reference(density, cotangent, adhesion):
    potential = jnp.stack([adhesion[0, 0] * density[0] + adhesion[0, 1] * density[1], adhesion[1, 0] * density[0] + adhesion[1, 1] * density[1]])

    def per_population(inputs):
        own_density, own_potential, own_cotangent = inputs
        updated, pullback = jax.vjp(adhesion_step, own_density, own_potential)
        return pullback(own_cotangent)
    direct, potential_bar = lax.map(per_population, (density, potential, cotangent))
    return jnp.stack([direct[0] + adhesion[0, 0] * potential_bar[0] + adhesion[1, 0] * potential_bar[1], direct[1] + adhesion[0, 1] * potential_bar[0] + adhesion[1, 1] * potential_bar[1]])
```

```python
import jax
import jax.numpy as jnp
import numpy as np
from jax import lax
from jax.experimental import pallas as pl
from jax.experimental.pallas import tpu as pltpu
from jax.sharding import PartitionSpec as P


R = 16
W = R + 1
NX = 16
NY = 32
NZ = 128
f32 = jnp.float32
bf16 = jnp.bfloat16

SMOOTH2 = 0.01
STEP = 0.5

offs = np.arange(-R, R + 1).astype(np.float64)
even_norm = np.sqrt(np.sum((W - np.abs(offs)) ** 2))
odd_norm = np.sqrt(np.sum((offs * (W - np.abs(offs))) ** 2))
SCALE = float(1.0 / (even_norm * even_norm * odd_norm))


def even(d):
    return np.where(np.abs(d) <= R, W - np.abs(d), 0).astype(np.float32)


def odd(d):
    return np.where(np.abs(d) <= R, d * (W - np.abs(d)), 0).astype(np.float32)


def y_matrix():
    lines = np.full(80, 10**6)
    lines[0:64] = np.arange(-16, 48)
    lines[64] = -17
    lines[65] = 48
    m = np.zeros((80, 80), np.float32)
    for c in range(NY):
        m[c] = even(lines - c)
    for j in range(NY + 1):
        m[NY + j] = odd(lines - (j - 1)) + odd(lines - j)
    return np.concatenate([m, m], 1)


def y_transposed():
    k = np.arange(-16, 48)[:, None]
    c = np.arange(NY)[None, :]
    m = np.concatenate([even(k - c), odd(k - c)], 1)
    return np.concatenate([m, m], 1)


def z_matrices():
    k = np.arange(NZ)[:, None]
    j = np.arange(NZ)[None, :]
    ze = even(k - j)
    zo = odd(k - j) + odd(k - j - 1)
    zo[:, NZ - 1] = 0
    return [np.concatenate([m, m], 0) for m in (ze, zo, zo.T)]


def split(x):
    hi = x.astype(bf16)
    lo = (x - hi.astype(f32)).astype(bf16)
    return hi, lo


def dot(a, b):
    return jnp.dot(a, b, preferred_element_type=f32)


def dot_rows(x, m):
    hi, lo = split(x)
    return dot(jnp.concatenate([hi, lo], 1), m)


YROWS = 576
CROWS = 544 * 2 + 64


def scalars_kernel(info, adh, info_out, adh_out):
    for i in range(5):
        info_out[i] = info[i]
    for i in range(2):
        for j in range(2):
            adh_out[i, j] = adh[i, j]


def pack_kernel(d, c, up, dn):
    for n in range(32):
        up[n * 16 : n * 16 + 16, :] = d[n * 32 + 16 : n * 32 + 32, :]
        dn[n * 16 : n * 16 + 16, :] = d[n * 32 : n * 32 + 16, :]
    up[512:544, :] = d[pl.ds(15, 32, stride=32), :]
    dn[512:544, :] = d[pl.ds(16, 32, stride=32), :]
    up[544:576, :] = c[pl.ds(31, 32, stride=32), :]
    dn[544:576, :] = c[pl.ds(0, 32, stride=32), :]


def corner_kernel(info, d, c, yl, yr, ma, mb, e0, e15):
    edge = info[0]
    for ref in (ma, mb):
        ref[0:544, :] = yl[0:544, :]
        ref[544:1088, :] = yr[0:544, :]
    for p in range(2):
        near = pl.multiple_of(p * 512 + (1 - edge) * 480, 32)
        far = pl.multiple_of(p * 512 + edge * 480, 32)
        r = 1088 + p * 32
        ma[r : r + 32, :] = c[pl.ds(near, 32), :]
        mb[r : r + 32, :] = c[pl.ds(far, 32), :]
        for ref, x in ((e0, 0), (e15, NX - 1)):
            n = p * 16 + x
            ref[p * 64 : p * 64 + 16, :] = yl[n * 16 : n * 16 + 16, :]
            ref[p * 64 + 16 : p * 64 + 48, :] = d[n * 32 : n * 32 + 32, :]
            ref[p * 64 + 48 : p * 64 + 64, :] = yr[n * 16 : n * 16 + 16, :]


def face(f, dl, du, cl, cu, valid):
    g = f * f + SMOOTH2
    r = lax.rsqrt(g)
    mag = g * r
    fb = (0.5 * STEP) * (cu - cl)
    if valid is not None:
        fb = jnp.where(valid, fb, 0.0)
    lower = fb * (f + mag)
    upper = fb * (f - mag)
    vb = fb * ((dl + du) - (f * r) * (du - dl))
    return lower, upper, vb


def main_kernel(
    info, adh, d, c, yl, yr, ba, bb, ka, kb, r2l, r2r, my, ze, zo, zot, myt,
    base, own, low, high, ga, gb, ha, hb,
    se, so, s1, s2, xo, xe, xy, dy, cy, tly, vby, wx, wy, wz, edges, ext, gm, hm,
):
    odd_core = info[0]
    left, right = info[1], info[2]
    below, above = info[3], info[4]

    a00, a01, a10, a11 = adh[0, 0], adh[0, 1], adh[1, 0], adh[1, 1]
    mat = my[...]

    def y_filter(parts):
        both = jnp.concatenate(
            [a00 * parts[0] + a01 * parts[1], a10 * parts[0] + a11 * parts[1]], 1
        )
        hi, lo = split(both)
        return dot(mat, jnp.concatenate([hi, lo], 0))

    ext[...] = jnp.zeros((1536, 128), f32)
    blocks = (
        (d, yl, 0, yr, 0, 16),
        (ba, ka, 0, ka, 544, 32 - 32 * odd_core),
        (bb, kb, 0, kb, 544, 32 * odd_core),
    )
    for i, (blk, kl, ol, kr, oh, first) in enumerate(blocks):
        ext[pl.ds(i * 512, 32, stride=16), :] = kl[ol + 512 : ol + 544, :]
        ext[pl.ds(i * 512 + 1, 32, stride=16), :] = kr[oh + 512 : oh + 544, :]
        for x in range(NX):
            parts = []
            for p in range(2):
                n = p * 16 + x
                r = i * 512 + n * 16
                parts.append(
                    jnp.concatenate(
                        [
                            kl[ol + n * 16 : ol + n * 16 + 16, :],
                            blk[n * 32 : n * 32 + 32, :],
                            kr[oh + n * 16 : oh + n * 16 + 16, :],
                            ext[r : r + 16, :],
                        ],
                        0,
                    )
                )
            out = y_filter(parts)
            for p in range(2):
                z = slice(p * 128, p * 128 + 128)
                re = (first + 1 + x) * 64 + p * 32
                ro = (first + x) * 80 + p * 40
                if i:
                    re, ro = pl.multiple_of(re, 32), pl.multiple_of(ro, 8)
                se[pl.ds(re, 32), :] = out[0:32, z]
                so[pl.ds(ro, 40), :] = out[32:72, z]
    for ref, q in ((r2l, 0), (r2r, 49)):
        zero16 = jnp.zeros((16, 128), f32)
        parts = [jnp.concatenate([ref[p * 64 : p * 64 + 64, :], zero16], 0) for p in range(2)]
        out = y_filter(parts)
        for p in range(2):
            se[q * 64 + p * 32 : q * 64 + p * 32 + 32, :] = out[0:32, p * 128 : p * 128 + 128]
    for ref, kref, side in ((ba, ka, 1 - odd_core), (bb, kb, odd_core)):
        q = pl.multiple_of(side * 128, 128)
        for p in range(2):
            src = pl.multiple_of(p * 512 + (1 - side) * 480, 32)
            edges[pl.ds(q + p * 32, 32), :] = ref[pl.ds(src, 32), :]
        edges[pl.ds(q + 64, 64), :] = kref[1088:1152, :]

    def pe(plane):
        q = (plane + 17) * 64
        return se[q : q + 64, :]

    def po(plane):
        q = (plane + 16) * 80
        return so[q : q + 80, :]

    b = pe(-17)
    for k in range(-16, 0):
        b = b + pe(k)
    t = None
    for j in range(1, 9):
        term = float(j) * (pe(-9 + j) - pe(-9 - j))
        t = term if t is None else t + term
    s2[0:64, :] = t
    for m in range(-9, 24):
        new, old = pe(m + 9), pe(m - 8)
        t = t + (8.0 * (new + old) + (old - b))
        s2[(m + 10) * 64 : (m + 11) * 64, :] = t
        if m < 23:
            b = b + (new - old)
            s1[(m + 9) * 64 : (m + 10) * 64, :] = b
    e = s1[0:64, :]
    for m in range(1, 17):
        e = e + s1[m * 64 : m * 64 + 64, :]
    xe[0:64, :] = e
    for k in range(15):
        e = e + (s1[(k + 17) * 64 : (k + 18) * 64, :] - s1[k * 64 : k * 64 + 64, :])
        xe[(k + 1) * 64 : (k + 2) * 64, :] = e
    o = s2[0:64, :]
    for m in range(1, 17):
        o = o + s2[m * 64 : m * 64 + 64, :]
    for j in range(17):
        nxt = o + (s2[(j + 17) * 64 : (j + 18) * 64, :] - s2[j * 64 : j * 64 + 64, :])
        xo[j * 64 : j * 64 + 64, :] = o + nxt
        o = nxt
    b = po(-16)
    for k in range(-15, 1):
        b = b + po(k)
    s1[0:80, :] = b
    for m in range(-8, 23):
        b = b + (po(m + 9) - po(m - 8))
        s1[(m + 9) * 80 : (m + 10) * 80, :] = b
    e = s1[0:80, :]
    for m in range(1, 17):
        e = e + s1[m * 80 : m * 80 + 80, :]
    xy[0:80, :] = e
    for k in range(15):
        e = e + (s1[(k + 17) * 80 : (k + 18) * 80, :] - s1[k * 80 : k * 80 + 80, :])
        xy[(k + 1) * 80 : (k + 2) * 80, :] = e

    mze, mzo, mzot = ze[...], zo[...], zot[...]
    for r in range(0, 1088, 64):
        xo[r : r + 64, :] = dot_rows(xo[r : r + 64, :], mze)
    for r in range(0, 1280, 80):
        xy[r : r + 80, :] = dot_rows(xy[r : r + 80, :], mze)
    for r in range(0, 1024, 64):
        xe[r : r + 64, :] = dot_rows(xe[r : r + 64, :], mzo)

    for p in range(2):
        prev_upper = prev_vb = None
        for j in range(17):
            f = SCALE * xo[j * 64 + p * 32 : j * 64 + p * 32 + 32, :]
            lo = p * 512 + (j - 1) * 32
            hi = p * 512 + j * 32
            dl = edges[p * 32 : p * 32 + 32, :] if j == 0 else d[lo : lo + 32, :]
            cl = edges[64 + p * 32 : 96 + p * 32, :] if j == 0 else c[lo : lo + 32, :]
            du = edges[128 + p * 32 : 160 + p * 32, :] if j == 16 else d[hi : hi + 32, :]
            cu = edges[192 + p * 32 : 224 + p * 32, :] if j == 16 else c[hi : hi + 32, :]
            valid = {0: left, 16: right}.get(j)
            lower, upper, vb = face(f, dl, du, cl, cu, None if valid is None else valid == 1)
            if j:
                base[lo : lo + 32, :] = cl + (lower + prev_upper)
                r = (j - 1) * 64 + p * 32
                wx[r : r + 32, :] = vb + prev_vb
            prev_upper, prev_vb = upper, vb

    for p in range(2):
        q = p * 16
        dy[pl.ds(p * 48 + 7, 16, stride=96), :] = yl[pl.ds(p * 256 + 15, 16, stride=16), :]
        dy[pl.ds(p * 48 + 40, 16, stride=96), :] = yr[pl.ds(p * 256, 16, stride=16), :]
        cy[pl.ds(p * 48 + 7, 16, stride=96), :] = yl[544 + q : 560 + q, :]
        cy[pl.ds(p * 48 + 40, 16, stride=96), :] = yr[544 + q : 560 + q, :]
        for x in range(NX):
            s = p * 512 + x * 32
            t = (x * 2 + p) * 48 + 8
            dy[t : t + 32, :] = d[s : s + 32, :]
            cy[t : t + 32, :] = c[s : s + 32, :]
    row = lax.broadcasted_iota(jnp.int32, (40, 128), 0)
    valid_y = ((row > 0) | (below == 1)) & ((row < 32) | (above == 1))
    lane = lax.broadcasted_iota(jnp.int32, (32, 128), 1)
    valid_z = lane < NZ - 1
    for x in range(NX):
        for p in range(2):
            n = x * 2 + p
            t = n * 48
            f = (0.5 * SCALE) * xy[n * 40 : n * 40 + 40, :]
            lower, upper, vb = face(
                f,
                dy[t + 7 : t + 47, :],
                dy[t + 8 : t + 48, :],
                cy[t + 7 : t + 47, :],
                cy[t + 8 : t + 48, :],
                valid_y,
            )
            tly[n * 40 : n * 40 + 40, :] = lower
            vby[n * 40 : n * 40 + 40, :] = vb
            s = p * 512 + x * 32
            f = (0.5 * SCALE) * xe[n * 32 : n * 32 + 32, :]
            dl, cl = d[s : s + 32, :], c[s : s + 32, :]
            du, cu = pltpu.roll(dl, NZ - 1, 1), pltpu.roll(cl, NZ - 1, 1)
            lower_z, upper_z, vb_z = face(f, dl, du, cl, cu, valid_z)
            wz[n * 32 : n * 32 + 32, :] = vb_z
            base[s : s + 32, :] = (
                base[s : s + 32, :] + upper[0:32, :] + (lower_z + pltpu.roll(upper_z, 1, 1))
            )
    for x in range(NX):
        for p in range(2):
            n = x * 2 + p
            s = p * 512 + x * 32
            base[s : s + 32, :] = base[s : s + 32, :] + tly[n * 40 + 1 : n * 40 + 33, :]
            wy[n * 32 : n * 32 + 32, :] = vby[n * 40 : n * 40 + 32, :] + vby[n * 40 + 1 : n * 40 + 33, :]

    for r in range(0, 1024, 64):
        wx[r : r + 64, :] = dot_rows(wx[r : r + 64, :], mze)
        wy[r : r + 64, :] = dot_rows(wy[r : r + 64, :], mze)
        wz[r : r + 64, :] = dot_rows(wz[r : r + 64, :], mzot)

    zero = jnp.zeros((64, 128), f32)

    def at(ref, plane):
        if 0 <= plane < NX:
            return ref[plane * 64 : plane * 64 + 64, :]
        return zero

    bx, t, bz, by = zero, zero, zero, zero
    for m in range(-9, 23):
        new, old = at(wx, m + 9), at(wx, m - 8)
        t = t + (8.0 * (new + old) + (old - bx))
        bx = bx + (new - old)
        bz = bz + (at(wz, m + 9) - at(wz, m - 8))
        by = by + (at(wy, m + 9) - at(wy, m - 8))
        q = (m + 9) * 64
        s1[q : q + 64, :] = bz - 2.0 * t
        s2[q : q + 64, :] = by

    def at2(ref, i):
        if 0 <= i < 32:
            return ref[i * 64 : i * 64 + 64, :]
        return zero

    matt = myt[...]
    ge, go = zero, zero
    for k in range(48):
        ge = ge + (at2(s1, k) - at2(s1, k - 17))
        go = go + (at2(s2, k) - at2(s2, k - 17))
        both = jnp.concatenate(
            [jnp.concatenate([ge[r : r + 32], go[r : r + 32]], 0) for r in (0, 32)], 1
        )
        hi, lo = split(both)
        out = dot(matt, jnp.concatenate([hi, lo], 0))
        for p in range(2):
            z = slice(p * 128, p * 128 + 128)
            if 16 <= k < 32:
                n = (k - 16) * 2 + p
                low[n * 16 : n * 16 + 16, :] = out[0:16, z]
                own[n * 32 : n * 32 + 32, :] = out[16:48, z]
                high[n * 16 : n * 16 + 16, :] = out[48:64, z]
            else:
                n = (k if k < 16 else k - 16) * 2 + p
                hm[n * 32 : n * 32 + 16, :] = out[0:16, z]
                gm[n * 32 : n * 32 + 32, :] = out[16:48, z]
                hm[n * 32 + 16 : n * 32 + 32, :] = out[48:64, z]
    to_a = pl.ds(pl.multiple_of((1 - odd_core) * 1024, 1024), 1024)
    to_b = pl.ds(pl.multiple_of(odd_core * 1024, 1024), 1024)
    ha[...] = hm[to_a, :]
    hb[...] = hm[to_b, :]
    ga[...] = gm[to_a, :]
    gb[...] = gm[to_b, :]


def margin_kernel(low, high, ha, hb, dn, up):
    for n in range(32):
        r, q = n * 16, n * 32
        dn[r : r + 16, :] = low[r : r + 16, :] + (ha[q : q + 16, :] + hb[q : q + 16, :])
        up[r : r + 16, :] = high[r : r + 16, :] + (ha[q + 16 : q + 32, :] + hb[q + 16 : q + 32, :])


def final_kernel(adh, base, own, ga, gb, yl, yr, out):
    h = 0.5 * SCALE
    for x in range(NX):
        pb = []
        for p in range(2):
            q = x * 32 + p * 16
            r = 2 * q
            got = jnp.concatenate([yl[q : q + 16, :], yr[q : q + 16, :]], 0)
            pb.append(own[r : r + 32, :] + (ga[r : r + 32, :] + gb[r : r + 32, :]) + got)
        for p in range(2):
            s = p * 512 + x * 32
            out[s : s + 32, :] = base[s : s + 32, :] + (
                (h * adh[0, p]) * pb[0] + (h * adh[1, p]) * pb[1]
            )


def rows(n):
    return jax.ShapeDtypeStruct((n, 128), f32)


def scratch(n):
    return pltpu.VMEM((n, 128), f32)


def call(kernel, smem, args, out_rows, scratch_rows=()):
    spec = pl.BlockSpec(memory_space=pltpu.VMEM)
    in_rows = sum(a.shape[0] for a in args[smem:])
    total = in_rows + sum(out_rows) + sum(scratch_rows)
    outs = [spec] * len(out_rows)
    shapes = [rows(n) for n in out_rows]
    single = len(out_rows) == 1
    return pl.pallas_call(
        kernel,
        out_shape=shapes[0] if single else shapes,
        in_specs=[pl.BlockSpec(memory_space=pltpu.SMEM)] * smem + [spec] * (len(args) - smem),
        out_specs=outs[0] if single else outs,
        scratch_shapes=[scratch(n) for n in scratch_rows],
        compiler_params=pltpu.CompilerParams(vmem_limit_bytes=total * 512 + (2 << 20)),
    )(*args)


def shift(values, axis, by):
    n = lax.axis_size(axis)
    pairs = [(i, i + by) for i in range(n) if 0 <= i + by < n]
    return lax.ppermute(values, axis, pairs)


def swap(values, first):
    n = lax.axis_size("gx")
    pairs = []
    for i in range(first, n - 1, 2):
        pairs += [(i, i + 1), (i + 1, i)]
    return lax.ppermute(values, "gx", pairs)


def step(density, cotangent, adhesion):
    gx, gy = lax.axis_index("gx"), lax.axis_index("gy")
    nx, ny = lax.axis_size("gx"), lax.axis_size("gy")
    info = jnp.stack([gx % 2, gx > 0, gx < nx - 1, gy > 0, gy < ny - 1]).astype(jnp.int32)
    smem = pl.BlockSpec(memory_space=pltpu.SMEM)
    info, adhesion = pl.pallas_call(
        scalars_kernel,
        out_shape=[
            jax.ShapeDtypeStruct((5,), jnp.int32),
            jax.ShapeDtypeStruct((2, 2), f32),
        ],
        in_specs=[smem, smem],
        out_specs=[smem, smem],
        compiler_params=pltpu.CompilerParams(vmem_limit_bytes=1 << 20),
    )(info, adhesion)
    my = jnp.asarray(y_matrix(), bf16)
    myt = jnp.asarray(y_transposed(), bf16)
    ze, zo, zot = (jnp.asarray(m, bf16) for m in z_matrices())
    d = density.reshape(1024, 128)
    c = cotangent.reshape(1024, 128)

    up, dn = call(pack_kernel, 0, [d, c], [YROWS, YROWS])
    yl = shift(up, "gy", 1)
    yr = shift(dn, "gy", -1)
    bb = swap(d, 1)
    ba = swap(d, 0)
    ma, mb, e0, e15 = call(
        corner_kernel, 1, [info, d, c, yl, yr], [CROWS, CROWS, 128, 128]
    )
    kb = swap(mb, 1)
    ka = swap(ma, 0)
    r2l = shift(e15, "gx", 2)
    r2r = shift(e0, "gx", -2)
    base, own, low, high, ga, gb, ha, hb = call(
        main_kernel,
        2,
        [info, adhesion, d, c, yl, yr, ba, bb, ka, kb, r2l, r2r, my, ze, zo, zot, myt],
        [1024, 1024, 512, 512, 1024, 1024, 1024, 1024],
        [
            50 * 64, 48 * 80, 32 * 80, 34 * 64, 17 * 64, 16 * 64, 16 * 80,
            32 * 48, 32 * 48, 32 * 40, 32 * 40, 1024, 1024, 1024, 256, 1536, 2048, 2048,
        ],
    )
    hb2 = swap(hb, 1)
    ha2 = swap(ha, 0)
    gb2 = swap(gb, 1)
    ga2 = swap(ga, 0)
    dn2, up2 = call(margin_kernel, 0, [low, high, ha2, hb2], [512, 512])
    yl2 = shift(up2, "gy", 1)
    yr2 = shift(dn2, "gy", -1)
    out = call(final_kernel, 1, [adhesion, base, own, ga2, gb2, yl2, yr2], [1024])
    return out.reshape(density.shape)


def solution(mesh):
    return jax.shard_map(
        step,
        mesh=mesh,
        in_specs=(P(None, "gx", "gy", None), P(None, "gx", "gy", None), P()),
        out_specs=P(None, "gx", "gy", None),
        check_vma=False,
    )
```

```python
import jax
import jax.numpy as jnp
import numpy as np
from jax import lax
from jax.experimental import pallas as pl
from jax.experimental.pallas import tpu as pltpu
from jax.sharding import PartitionSpec as P


R = 16
W = R + 1
NX = 16
NY = 32
NZ = 128
f32 = jnp.float32
bf16 = jnp.bfloat16

SMOOTH2 = 0.01
STEP = 0.5

offs = np.arange(-R, R + 1).astype(np.float64)
even_norm = np.sqrt(np.sum((W - np.abs(offs)) ** 2))
odd_norm = np.sqrt(np.sum((offs * (W - np.abs(offs))) ** 2))
SCALE = float(1.0 / (even_norm * even_norm * odd_norm))


def even(d):
    return np.where(np.abs(d) <= R, W - np.abs(d), 0).astype(np.float32)


def odd(d):
    return np.where(np.abs(d) <= R, d * (W - np.abs(d)), 0).astype(np.float32)


def y_matrix():
    lines = np.full(80, 10**6)
    lines[0:64] = np.arange(-16, 48)
    lines[64] = -17
    lines[65] = 48
    m = np.zeros((80, 80), np.float32)
    for c in range(NY):
        m[c] = even(lines - c)
    for j in range(NY + 1):
        m[NY + j] = odd(lines - (j - 1)) + odd(lines - j)
    return np.concatenate([m, m], 1)


def y_transposed():
    k = np.arange(-16, 48)[:, None]
    c = np.arange(NY)[None, :]
    m = np.concatenate([even(k - c), odd(k - c)], 1)
    return np.concatenate([m, m], 1)


def z_matrices():
    k = np.arange(NZ)[:, None]
    j = np.arange(NZ)[None, :]
    ze = even(k - j)
    zo = odd(k - j) + odd(k - j - 1)
    zo[:, NZ - 1] = 0
    return [np.concatenate([m, m], 0) for m in (ze, zo, zo.T)]


def split(x):
    hi = x.astype(bf16)
    lo = (x - hi.astype(f32)).astype(bf16)
    return hi, lo


def dot(a, b):
    return jnp.dot(a, b, preferred_element_type=f32)


def dot_rows(x, m):
    hi, lo = split(x)
    return dot(jnp.concatenate([hi, lo], 1), m)


YROWS = 576
CROWS = 544 * 2 + 64


def spread_kernel(adh, out):
    for i in range(2):
        for j in range(2):
            out[i * 16 + j * 8 : i * 16 + j * 8 + 8, :] = jnp.full((8, 128), adh[i, j], f32)


def adhesion_rows(av):
    return [av[i * 8 : i * 8 + 1, :] for i in range(4)]


def pack_kernel(d, c, up, dn, dv, cv, sems):
    copies = []
    for i, (src, dst) in enumerate(((d, dv), (c, cv))):
        for k in range(4):
            part = pl.ds(k * 256, 256)
            copies.append(pltpu.make_async_copy(src.at[part], dst.at[part], sems.at[i * 4 + k]))
    for copy in copies:
        copy.start()
    for copy in copies[:4]:
        copy.wait()
    for n in range(32):
        up[n * 16 : n * 16 + 16, :] = dv[n * 32 + 16 : n * 32 + 32, :]
        dn[n * 16 : n * 16 + 16, :] = dv[n * 32 : n * 32 + 16, :]
    up[512:544, :] = dv[pl.ds(15, 32, stride=32), :]
    dn[512:544, :] = dv[pl.ds(16, 32, stride=32), :]
    for copy in copies[4:]:
        copy.wait()
    up[544:576, :] = cv[pl.ds(31, 32, stride=32), :]
    dn[544:576, :] = cv[pl.ds(0, 32, stride=32), :]


def corner_kernel(av, d, c, yl, yr, ma, mb, e0, e15):
    edge = lax.rem(lax.axis_index("gx"), 2)
    for ref in (ma, mb):
        ref[0:544, :] = yl[0:544, :]
        ref[544:1088, :] = yr[0:544, :]
    for p in range(2):
        near = pl.multiple_of(p * 512 + (1 - edge) * 480, 32)
        far = pl.multiple_of(p * 512 + edge * 480, 32)
        r = 1088 + p * 32
        ma[r : r + 32, :] = c[pl.ds(near, 32), :]
        mb[r : r + 32, :] = c[pl.ds(far, 32), :]
        for ref, x in ((e0, 0), (e15, NX - 1)):
            n = p * 16 + x
            ref[p * 64 : p * 64 + 16, :] = yl[n * 16 : n * 16 + 16, :]
            ref[p * 64 + 16 : p * 64 + 48, :] = d[n * 32 : n * 32 + 32, :]
            ref[p * 64 + 48 : p * 64 + 64, :] = yr[n * 16 : n * 16 + 16, :]


def face_bar(f, dl, du, cl, cu, valid):
    r = lax.rsqrt(f * f + SMOOTH2)
    fb = (0.5 * STEP) * (cu - cl)
    if valid is not None:
        fb = jnp.where(valid, fb, 0.0)
    return fb * ((dl + du) - (f * r) * (du - dl))


def face_sides(f, cl, cu, valid):
    g = f * f + SMOOTH2
    mag = g * lax.rsqrt(g)
    fb = (0.5 * STEP) * (cu - cl)
    if valid is not None:
        fb = jnp.where(valid, fb, 0.0)
    return fb * (f + mag), fb * (f - mag)


def y_filter(mat, av, parts):
    a00, a01, a10, a11 = adhesion_rows(av)
    both = jnp.concatenate(
        [a00 * parts[0] + a01 * parts[1], a10 * parts[0] + a11 * parts[1]], 1
    )
    hi, lo = split(both)
    return dot(mat, jnp.concatenate([hi, lo], 0))


def y_filter_block(mat, av, blk, kl, ol, kr, oh, ext, store):
    ext[...] = jnp.zeros((512, 128), f32)
    ext[pl.ds(0, 32, stride=16), :] = kl[ol + 512 : ol + 544, :]
    ext[pl.ds(1, 32, stride=16), :] = kr[oh + 512 : oh + 544, :]
    for x in range(NX):
        parts = []
        for p in range(2):
            n = p * 16 + x
            parts.append(
                jnp.concatenate(
                    [
                        kl[ol + n * 16 : ol + n * 16 + 16, :],
                        blk[n * 32 : n * 32 + 32, :],
                        kr[oh + n * 16 : oh + n * 16 + 16, :],
                        ext[n * 16 : n * 16 + 16, :],
                    ],
                    0,
                )
            )
        out = y_filter(mat, av, parts)
        for p in range(2):
            z = slice(p * 128, p * 128 + 128)
            store(x, p, out[0:32, z], out[32:72, z])


def y_own_kernel(av, d, yl, yr, my, seo, soo, ext):
    def store(x, p, e, o):
        n = x * 2 + p
        seo[n * 32 : n * 32 + 32, :] = e
        soo[n * 40 : n * 40 + 40, :] = o

    y_filter_block(my[...], av, d, yl, 0, yr, 0, ext, store)


def masks(axis):
    i, n = lax.axis_index(axis), lax.axis_size(axis)
    return i > 0, i < n - 1


def y_mask():
    below, above = masks("gy")
    row = lax.broadcasted_iota(jnp.int32, (40, 128), 0)
    first = jnp.where(below, 0, 1)
    last = jnp.where(above, 32, 31)
    return (row >= first) & (row <= last)


def z_mask():
    return lax.broadcasted_iota(jnp.int32, (32, 128), 1) < NZ - 1


def x_face_cells(edges, d, p, j, base):
    lo, hi = p * 512 + (j - 1) * 32, p * 512 + j * 32
    low = edges[base + p * 32 : base + p * 32 + 32, :] if j == 0 else d[lo : lo + 32, :]
    r = 128 + base + p * 32
    high = edges[r : r + 32, :] if j == 16 else d[hi : hi + 32, :]
    return low, high


def main_kernel(
    av, d, c, yl, yr, ba, bb, ka, kb, r2l, r2r, seo, soo, my, ze, zo, zot, myt,
    own, low, high, am, gb, hb, xo, xe, xy, dy, cy, edges,
    se, so, s1, s2, vby, wx, wy, wz, ext, gm, hm,
):
    odd_core = lax.rem(lax.axis_index("gx"), 2)
    left, right = masks("gx")

    mat = my[...]
    for blk, k, side in ((ba, ka, 1 - odd_core), (bb, kb, odd_core)):

        def store(x, p, e, o, side=side):
            se[pl.ds(pl.multiple_of((16 * side + 1 + x) * 64 + p * 32, 32), 32), :] = e
            so[pl.ds(pl.multiple_of((16 * side + x) * 80 + p * 40, 8), 40), :] = o

        y_filter_block(mat, av, blk, k, 0, k, 544, ext, store)
    for ref, q in ((r2l, 0), (r2r, 33)):
        zero16 = jnp.zeros((16, 128), f32)
        parts = [jnp.concatenate([ref[p * 64 : p * 64 + 64, :], zero16], 0) for p in range(2)]
        out = y_filter(mat, av, parts)
        for p in range(2):
            se[q * 64 + p * 32 : q * 64 + p * 32 + 32, :] = out[0:32, p * 128 : p * 128 + 128]
    for ref, kref, side in ((ba, ka, 1 - odd_core), (bb, kb, odd_core)):
        q = pl.multiple_of(side * 128, 128)
        for p in range(2):
            src = pl.multiple_of(p * 512 + (1 - side) * 480, 32)
            edges[pl.ds(q + p * 32, 32), :] = ref[pl.ds(src, 32), :]
        edges[pl.ds(q + 64, 64), :] = kref[1088:1152, :]

    def pe(plane):
        if 0 <= plane < NX:
            return seo[plane * 64 : plane * 64 + 64, :]
        q = (plane + 17 if plane < 0 else plane + 1) * 64
        return se[q : q + 64, :]

    def po(plane):
        if 0 <= plane < NX:
            return soo[plane * 80 : plane * 80 + 80, :]
        q = (plane + 16 if plane < 0 else plane) * 80
        return so[q : q + 80, :]

    b = pe(-17)
    for k in range(-16, 0):
        b = b + pe(k)
    t = None
    for j in range(1, 9):
        term = float(j) * (pe(-9 + j) - pe(-9 - j))
        t = term if t is None else t + term
    s2[0:64, :] = t
    for m in range(-9, 24):
        new, old = pe(m + 9), pe(m - 8)
        t = t + (8.0 * (new + old) + (old - b))
        s2[(m + 10) * 64 : (m + 11) * 64, :] = t
        if m < 23:
            b = b + (new - old)
            s1[(m + 9) * 64 : (m + 10) * 64, :] = b
    e = s1[0:64, :]
    for m in range(1, 17):
        e = e + s1[m * 64 : m * 64 + 64, :]
    xe[0:64, :] = e
    for k in range(15):
        e = e + (s1[(k + 17) * 64 : (k + 18) * 64, :] - s1[k * 64 : k * 64 + 64, :])
        xe[(k + 1) * 64 : (k + 2) * 64, :] = e
    o = s2[0:64, :]
    for m in range(1, 17):
        o = o + s2[m * 64 : m * 64 + 64, :]
    for j in range(17):
        nxt = o + (s2[(j + 17) * 64 : (j + 18) * 64, :] - s2[j * 64 : j * 64 + 64, :])
        xo[j * 64 : j * 64 + 64, :] = o + nxt
        o = nxt
    b = po(-16)
    for k in range(-15, 1):
        b = b + po(k)
    s1[0:80, :] = b
    for m in range(-8, 23):
        b = b + (po(m + 9) - po(m - 8))
        s1[(m + 9) * 80 : (m + 10) * 80, :] = b
    e = s1[0:80, :]
    for m in range(1, 17):
        e = e + s1[m * 80 : m * 80 + 80, :]
    xy[0:80, :] = e
    for k in range(15):
        e = e + (s1[(k + 17) * 80 : (k + 18) * 80, :] - s1[k * 80 : k * 80 + 80, :])
        xy[(k + 1) * 80 : (k + 2) * 80, :] = e

    mze, mzo, mzot = ze[...], zo[...], zot[...]
    for r in range(0, 1088, 64):
        xo[r : r + 64, :] = dot_rows(xo[r : r + 64, :], mze)
    for r in range(0, 1280, 80):
        xy[r : r + 80, :] = dot_rows(xy[r : r + 80, :], mze)
    for r in range(0, 1024, 64):
        xe[r : r + 64, :] = dot_rows(xe[r : r + 64, :], mzo)

    for p in range(2):
        prev = None
        for j in range(17):
            f = SCALE * xo[j * 64 + p * 32 : j * 64 + p * 32 + 32, :]
            dl, du = x_face_cells(edges, d, p, j, 0)
            cl, cu = x_face_cells(edges, c, p, j, 64)
            vb = face_bar(f, dl, du, cl, cu, {0: left, 16: right}.get(j))
            if j:
                r = (j - 1) * 64 + p * 32
                wx[r : r + 32, :] = vb + prev
            prev = vb

    for p in range(2):
        q = p * 16
        dy[pl.ds(p * 48 + 7, 16, stride=96), :] = yl[pl.ds(p * 256 + 15, 16, stride=16), :]
        dy[pl.ds(p * 48 + 40, 16, stride=96), :] = yr[pl.ds(p * 256, 16, stride=16), :]
        cy[pl.ds(p * 48 + 7, 16, stride=96), :] = yl[544 + q : 560 + q, :]
        cy[pl.ds(p * 48 + 40, 16, stride=96), :] = yr[544 + q : 560 + q, :]
        for x in range(NX):
            s = p * 512 + x * 32
            t = (x * 2 + p) * 48 + 8
            dy[t : t + 32, :] = d[s : s + 32, :]
            cy[t : t + 32, :] = c[s : s + 32, :]
    valid_y, valid_z = y_mask(), z_mask()
    for x in range(NX):
        for p in range(2):
            n = x * 2 + p
            t = n * 48
            f = (0.5 * SCALE) * xy[n * 40 : n * 40 + 40, :]
            vby[n * 40 : n * 40 + 40, :] = face_bar(
                f,
                dy[t + 7 : t + 47, :],
                dy[t + 8 : t + 48, :],
                cy[t + 7 : t + 47, :],
                cy[t + 8 : t + 48, :],
                valid_y,
            )
            s = p * 512 + x * 32
            f = (0.5 * SCALE) * xe[n * 32 : n * 32 + 32, :]
            dl, cl = d[s : s + 32, :], c[s : s + 32, :]
            du, cu = pltpu.roll(dl, NZ - 1, 1), pltpu.roll(cl, NZ - 1, 1)
            wz[n * 32 : n * 32 + 32, :] = face_bar(f, dl, du, cl, cu, valid_z)
    for n in range(32):
        wy[n * 32 : n * 32 + 32, :] = vby[n * 40 : n * 40 + 32, :] + vby[n * 40 + 1 : n * 40 + 33, :]

    for r in range(0, 1024, 64):
        wx[r : r + 64, :] = dot_rows(wx[r : r + 64, :], mze)
        wy[r : r + 64, :] = dot_rows(wy[r : r + 64, :], mze)
        wz[r : r + 64, :] = dot_rows(wz[r : r + 64, :], mzot)

    zero = jnp.zeros((64, 128), f32)

    def at(ref, plane):
        if 0 <= plane < NX:
            return ref[plane * 64 : plane * 64 + 64, :]
        return zero

    bx, t, bz, by = zero, zero, zero, zero
    for m in range(-9, 23):
        new, old = at(wx, m + 9), at(wx, m - 8)
        t = t + (8.0 * (new + old) + (old - bx))
        bx = bx + (new - old)
        bz = bz + (at(wz, m + 9) - at(wz, m - 8))
        by = by + (at(wy, m + 9) - at(wy, m - 8))
        q = (m + 9) * 64
        s1[q : q + 64, :] = bz - 2.0 * t
        s2[q : q + 64, :] = by

    def at2(ref, i):
        if 0 <= i < 32:
            return ref[i * 64 : i * 64 + 64, :]
        return zero

    matt = myt[...]
    ge, go = zero, zero
    for k in range(48):
        ge = ge + (at2(s1, k) - at2(s1, k - 17))
        go = go + (at2(s2, k) - at2(s2, k - 17))
        both = jnp.concatenate(
            [jnp.concatenate([ge[r : r + 32], go[r : r + 32]], 0) for r in (0, 32)], 1
        )
        hi, lo = split(both)
        out = dot(matt, jnp.concatenate([hi, lo], 0))
        for p in range(2):
            z = slice(p * 128, p * 128 + 128)
            if 16 <= k < 32:
                n = (k - 16) * 2 + p
                low[n * 16 : n * 16 + 16, :] = out[0:16, z]
                own[n * 32 : n * 32 + 32, :] = out[16:48, z]
                high[n * 16 : n * 16 + 16, :] = out[48:64, z]
            else:
                n = (k if k < 16 else k - 16) * 2 + p
                hm[n * 32 : n * 32 + 16, :] = out[0:16, z]
                gm[n * 32 : n * 32 + 32, :] = out[16:48, z]
                hm[n * 32 + 16 : n * 32 + 32, :] = out[48:64, z]
    to_a = pl.ds(pl.multiple_of((1 - odd_core) * 1024, 1024), 1024)
    to_b = pl.ds(pl.multiple_of(odd_core * 1024, 1024), 1024)
    am[0:1024, :] = hm[to_a, :]
    am[1024:2048, :] = gm[to_a, :]
    hb[...] = hm[to_b, :]
    gb[...] = gm[to_b, :]


def base_kernel(d, c, xo, xe, xy, cy, edges, base, tly):
    left, right = masks("gx")
    for p in range(2):
        prev = None
        for j in range(17):
            f = SCALE * xo[j * 64 + p * 32 : j * 64 + p * 32 + 32, :]
            cl, cu = x_face_cells(edges, c, p, j, 64)
            lower, upper = face_sides(f, cl, cu, {0: left, 16: right}.get(j))
            if j:
                s = p * 512 + (j - 1) * 32
                base[s : s + 32, :] = cl + (lower + prev)
            prev = upper
    valid_y, valid_z = y_mask(), z_mask()
    for x in range(NX):
        for p in range(2):
            n = x * 2 + p
            t = n * 48
            f = (0.5 * SCALE) * xy[n * 40 : n * 40 + 40, :]
            lower, upper = face_sides(f, cy[t + 7 : t + 47, :], cy[t + 8 : t + 48, :], valid_y)
            tly[n * 40 : n * 40 + 40, :] = lower
            s = p * 512 + x * 32
            f = (0.5 * SCALE) * xe[n * 32 : n * 32 + 32, :]
            cl = c[s : s + 32, :]
            lower_z, upper_z = face_sides(f, cl, pltpu.roll(cl, NZ - 1, 1), valid_z)
            base[s : s + 32, :] = (
                base[s : s + 32, :] + upper[0:32, :] + (lower_z + pltpu.roll(upper_z, 1, 1))
            )
    for x in range(NX):
        for p in range(2):
            n = x * 2 + p
            s = p * 512 + x * 32
            base[s : s + 32, :] = base[s : s + 32, :] + tly[n * 40 + 1 : n * 40 + 33, :]


def margin_kernel(low, high, ha, hb, dn, up):
    for n in range(32):
        r, q = n * 16, n * 32
        dn[r : r + 16, :] = low[r : r + 16, :] + (ha[q : q + 16, :] + hb[q : q + 16, :])
        up[r : r + 16, :] = high[r : r + 16, :] + (ha[q + 16 : q + 32, :] + hb[q + 16 : q + 32, :])


def final_kernel(av, base, own, ga, gb, yl, yr, out):
    h = 0.5 * SCALE
    weights = [h * a for a in adhesion_rows(av)]
    for x in range(NX):
        pb = []
        for p in range(2):
            q = x * 32 + p * 16
            r = 2 * q
            got = jnp.concatenate([yl[q : q + 16, :], yr[q : q + 16, :]], 0)
            pb.append(own[r : r + 32, :] + (ga[1024 + r : 1056 + r, :] + gb[r : r + 32, :]) + got)
        for p in range(2):
            s = p * 512 + x * 32
            out[s : s + 32, :] = base[s : s + 32, :] + (
                weights[p] * pb[0] + weights[2 + p] * pb[1]
            )


def rows(n):
    return jax.ShapeDtypeStruct((n, 128), f32)


def scratch(n):
    return pltpu.VMEM((n, 128), f32)


def call(kernel, args, out_rows, scratch_rows=()):
    spec = pl.BlockSpec(memory_space=pltpu.VMEM)
    total = sum(a.shape[0] for a in args) + sum(out_rows) + sum(scratch_rows)
    single = len(out_rows) == 1
    shapes = [rows(n) for n in out_rows]
    return pl.pallas_call(
        kernel,
        out_shape=shapes[0] if single else shapes,
        in_specs=[spec] * len(args),
        out_specs=spec if single else [spec] * len(out_rows),
        scratch_shapes=[scratch(n) for n in scratch_rows],
        compiler_params=pltpu.CompilerParams(vmem_limit_bytes=total * 512 + (2 << 20)),
    )(*args)


def pack(d, c):
    spec = pl.BlockSpec(memory_space=pltpu.VMEM)
    return pl.pallas_call(
        pack_kernel,
        out_shape=[rows(YROWS), rows(YROWS), rows(1024), rows(1024)],
        in_specs=[pl.BlockSpec(memory_space=pltpu.HBM)] * 2,
        out_specs=[spec] * 4,
        scratch_shapes=[pltpu.SemaphoreType.DMA((8,))],
        compiler_params=pltpu.CompilerParams(vmem_limit_bytes=54_600_000),
    )(d, c)


def spread(adhesion):
    return pl.pallas_call(
        spread_kernel,
        out_shape=rows(32),
        in_specs=[pl.BlockSpec(memory_space=pltpu.SMEM)],
        out_specs=pl.BlockSpec(memory_space=pltpu.VMEM),
        compiler_params=pltpu.CompilerParams(vmem_limit_bytes=1 << 20),
    )(adhesion)


def shift(values, axis, by):
    n = lax.axis_size(axis)
    pairs = [(i, i + by) for i in range(n) if 0 <= i + by < n]
    return lax.ppermute(values, axis, pairs)


def swap(values, first):
    n = lax.axis_size("gx")
    pairs = []
    for i in range(first, n - 1, 2):
        pairs += [(i, i + 1), (i + 1, i)]
    return lax.ppermute(values, "gx", pairs)


def step(density, cotangent, adhesion):
    my = jnp.asarray(y_matrix(), bf16)
    myt = jnp.asarray(y_transposed(), bf16)
    ze, zo, zot = (jnp.asarray(m, bf16) for m in z_matrices())
    up, dn, d, c = pack(density.reshape(1024, 128), cotangent.reshape(1024, 128))
    yl = shift(up, "gy", 1)
    yr = shift(dn, "gy", -1)
    bb = swap(d, 1)
    ba = swap(d, 0)
    av = spread(adhesion)
    ma, mb, e0, e15 = call(
        corner_kernel, [av, d, c, yl, yr], [CROWS, CROWS, 128, 128]
    )
    kb = swap(mb, 1)
    ka = swap(ma, 0)
    r2l = shift(e15, "gx", 2)
    r2r = shift(e0, "gx", -2)
    seo, soo = call(y_own_kernel, [av, d, yl, yr, my], [1024, 1280], [512])
    own, low, high, am, gb, hb, xo, xe, xy, _, cy, edges = call(
        main_kernel,
        [av, d, c, yl, yr, ba, bb, ka, kb, r2l, r2r, seo, soo, my, ze, zo, zot, myt],
        [1024, 512, 512, 2048, 1024, 1024, 17 * 64, 1024, 1280, 1536, 1536, 256],
        [34 * 64, 32 * 80, 32 * 80, 34 * 64, 1280, 1024, 1024, 1024, 512, 2048, 2048],
    )
    hb2 = swap(hb, 1)
    gb2 = swap(gb, 1)
    am2 = swap(am, 0)
    dn2, up2 = call(margin_kernel, [low, high, am2, hb2], [512, 512])
    yl2 = shift(up2, "gy", 1)
    yr2 = shift(dn2, "gy", -1)
    base = call(base_kernel, [d, c, xo, xe, xy, cy, edges], [1024], [1280])
    out = call(final_kernel, [av, base, own, am2, gb2, yl2, yr2], [1024])
    return out.reshape(density.shape)


def solution(mesh):
    return jax.shard_map(
        step,
        mesh=mesh,
        in_specs=(P(None, "gx", "gy", None), P(None, "gx", "gy", None), P()),
        out_specs=P(None, "gx", "gy", None),
        check_vma=False,
    )
```

```python
import jax
import jax.numpy as jnp
import numpy as np
from jax import lax
from jax.experimental import pallas as pl
from jax.experimental.pallas import tpu as pltpu
from jax.sharding import PartitionSpec as P


R = 16
W = R + 1
NX = 16
NY = 32
NZ = 128
f32 = jnp.float32
bf16 = jnp.bfloat16

SMOOTH2 = 0.01
STEP = 0.5

offs = np.arange(-R, R + 1).astype(np.float64)
even_norm = np.sqrt(np.sum((W - np.abs(offs)) ** 2))
odd_norm = np.sqrt(np.sum((offs * (W - np.abs(offs))) ** 2))
SCALE = float(1.0 / (even_norm * even_norm * odd_norm))


def even(d):
    return np.where(np.abs(d) <= R, W - np.abs(d), 0).astype(np.float32)


def odd(d):
    return np.where(np.abs(d) <= R, d * (W - np.abs(d)), 0).astype(np.float32)


def y_matrix():
    lines = np.full(80, 10**6)
    lines[0:64] = np.arange(-16, 48)
    lines[64] = -17
    lines[65] = 48
    m = np.zeros((80, 80), np.float32)
    for c in range(NY):
        m[c] = even(lines - c)
    for j in range(NY + 1):
        m[NY + j] = odd(lines - (j - 1)) + odd(lines - j)
    return np.concatenate([m, m], 1)


def y_transposed():
    k = np.arange(-16, 48)[:, None]
    c = np.arange(NY)[None, :]
    m = np.concatenate([even(k - c), odd(k - c)], 1)
    return np.concatenate([m, m], 1)


def z_matrices():
    k = np.arange(NZ)[:, None]
    j = np.arange(NZ)[None, :]
    ze = even(k - j)
    zo = odd(k - j) + odd(k - j - 1)
    zo[:, NZ - 1] = 0
    return [np.concatenate([m, m], 0) for m in (ze, zo, zo.T)]


def split(x):
    hi = x.astype(bf16)
    lo = (x - hi.astype(f32)).astype(bf16)
    return hi, lo


def dot(a, b):
    return jnp.dot(a, b, preferred_element_type=f32)


def dot_rows(x, m):
    hi, lo = split(x)
    return dot(jnp.concatenate([hi, lo], 1), m)


YROWS = 576
CROWS = 544 * 2 + 64


def spread_kernel(adh, out):
    for i in range(2):
        for j in range(2):
            out[i * 16 + j * 8 : i * 16 + j * 8 + 8, :] = jnp.full((8, 128), adh[i, j], f32)


def adhesion_rows(av):
    return [av[i * 8 : i * 8 + 1, :] for i in range(4)]


def pack_kernel(d, c, up, dn, dv, cv, sems):
    copies = []
    for i, (src, dst) in enumerate(((d, dv), (c, cv))):
        for k in range(4):
            part = pl.ds(k * 256, 256)
            copies.append(pltpu.make_async_copy(src.at[part], dst.at[part], sems.at[i * 4 + k]))
    for copy in copies:
        copy.start()
    for copy in copies[:4]:
        copy.wait()
    for n in range(32):
        up[n * 16 : n * 16 + 16, :] = dv[n * 32 + 16 : n * 32 + 32, :]
        dn[n * 16 : n * 16 + 16, :] = dv[n * 32 : n * 32 + 16, :]
    up[512:544, :] = dv[pl.ds(15, 32, stride=32), :]
    dn[512:544, :] = dv[pl.ds(16, 32, stride=32), :]
    for copy in copies[4:]:
        copy.wait()
    up[544:576, :] = cv[pl.ds(31, 32, stride=32), :]
    dn[544:576, :] = cv[pl.ds(0, 32, stride=32), :]


def corner_kernel(av, d, c, yl, yr, ma, mb, e0, e15):
    edge = lax.rem(lax.axis_index("gx"), 2)
    for ref in (ma, mb):
        ref[0:544, :] = yl[0:544, :]
        ref[544:1088, :] = yr[0:544, :]
    for p in range(2):
        near = pl.multiple_of(p * 512 + (1 - edge) * 480, 32)
        far = pl.multiple_of(p * 512 + edge * 480, 32)
        r = 1088 + p * 32
        ma[r : r + 32, :] = c[pl.ds(near, 32), :]
        mb[r : r + 32, :] = c[pl.ds(far, 32), :]
        for ref, x in ((e0, 0), (e15, NX - 1)):
            n = p * 16 + x
            ref[p * 64 : p * 64 + 16, :] = yl[n * 16 : n * 16 + 16, :]
            ref[p * 64 + 16 : p * 64 + 48, :] = d[n * 32 : n * 32 + 32, :]
            ref[p * 64 + 48 : p * 64 + 64, :] = yr[n * 16 : n * 16 + 16, :]


def face_bar(f, dl, du, cl, cu, valid):
    r = lax.rsqrt(f * f + SMOOTH2)
    fb = (0.5 * STEP) * (cu - cl)
    if valid is not None:
        fb = jnp.where(valid, fb, 0.0)
    return fb * ((dl + du) - (f * r) * (du - dl))


def face_sides(f, cl, cu, valid):
    g = f * f + SMOOTH2
    mag = g * lax.rsqrt(g)
    fb = (0.5 * STEP) * (cu - cl)
    if valid is not None:
        fb = jnp.where(valid, fb, 0.0)
    return fb * (f + mag), fb * (f - mag)


def y_filter(mat, av, parts):
    a00, a01, a10, a11 = adhesion_rows(av)
    both = jnp.concatenate(
        [a00 * parts[0] + a01 * parts[1], a10 * parts[0] + a11 * parts[1]], 1
    )
    hi, lo = split(both)
    return dot(mat, jnp.concatenate([hi, lo], 0))


def y_filter_block(mat, av, blk, kl, ol, kr, oh, ext, store):
    ext[...] = jnp.zeros((512, 128), f32)
    ext[pl.ds(0, 32, stride=16), :] = kl[ol + 512 : ol + 544, :]
    ext[pl.ds(1, 32, stride=16), :] = kr[oh + 512 : oh + 544, :]
    for x in range(NX):
        parts = []
        for p in range(2):
            n = p * 16 + x
            parts.append(
                jnp.concatenate(
                    [
                        kl[ol + n * 16 : ol + n * 16 + 16, :],
                        blk[n * 32 : n * 32 + 32, :],
                        kr[oh + n * 16 : oh + n * 16 + 16, :],
                        ext[n * 16 : n * 16 + 16, :],
                    ],
                    0,
                )
            )
        out = y_filter(mat, av, parts)
        for p in range(2):
            z = slice(p * 128, p * 128 + 128)
            store(x, p, out[0:32, z], out[32:72, z])


def y_own_kernel(av, d, yl, yr, my, seo, soo, ext):
    def store(x, p, e, o):
        n = x * 2 + p
        seo[n * 32 : n * 32 + 32, :] = e
        soo[n * 40 : n * 40 + 40, :] = o

    y_filter_block(my[...], av, d, yl, 0, yr, 0, ext, store)


def masks(axis):
    i, n = lax.axis_index(axis), lax.axis_size(axis)
    return i > 0, i < n - 1


def y_mask():
    below, above = masks("gy")
    row = lax.broadcasted_iota(jnp.int32, (40, 128), 0)
    first = jnp.where(below, 0, 1)
    last = jnp.where(above, 32, 31)
    return (row >= first) & (row <= last)


def z_mask():
    return lax.broadcasted_iota(jnp.int32, (32, 128), 1) < NZ - 1


def x_face_cells(edges, d, p, j, base):
    lo, hi = p * 512 + (j - 1) * 32, p * 512 + j * 32
    low = edges[base + p * 32 : base + p * 32 + 32, :] if j == 0 else d[lo : lo + 32, :]
    r = 128 + base + p * 32
    high = edges[r : r + 32, :] if j == 16 else d[hi : hi + 32, :]
    return low, high


def main_kernel(
    av, d, c, yl, yr, ba, bb, ka, kb, r2l, r2r, seo, soo, my, ze, zo, zot, myt,
    own, low, high, am, gb, hb, xo, xe, xy, cy, edges,
    dy, se, so, s1, s2, vby, wx, wy, wz, ext, gm, hm,
):
    odd_core = lax.rem(lax.axis_index("gx"), 2)
    left, right = masks("gx")

    mat = my[...]
    for blk, k, side in ((ba, ka, 1 - odd_core), (bb, kb, odd_core)):

        def store(x, p, e, o, side=side):
            se[pl.ds(pl.multiple_of((16 * side + 1 + x) * 64 + p * 32, 32), 32), :] = e
            so[pl.ds(pl.multiple_of((16 * side + x) * 80 + p * 40, 8), 40), :] = o

        y_filter_block(mat, av, blk, k, 0, k, 544, ext, store)
    for ref, q in ((r2l, 0), (r2r, 33)):
        zero16 = jnp.zeros((16, 128), f32)
        parts = [jnp.concatenate([ref[p * 64 : p * 64 + 64, :], zero16], 0) for p in range(2)]
        out = y_filter(mat, av, parts)
        for p in range(2):
            se[q * 64 + p * 32 : q * 64 + p * 32 + 32, :] = out[0:32, p * 128 : p * 128 + 128]
    for ref, kref, side in ((ba, ka, 1 - odd_core), (bb, kb, odd_core)):
        q = pl.multiple_of(side * 128, 128)
        for p in range(2):
            src = pl.multiple_of(p * 512 + (1 - side) * 480, 32)
            edges[pl.ds(q + p * 32, 32), :] = ref[pl.ds(src, 32), :]
        edges[pl.ds(q + 64, 64), :] = kref[1088:1152, :]

    def pe(plane):
        if 0 <= plane < NX:
            return seo[plane * 64 : plane * 64 + 64, :]
        q = (plane + 17 if plane < 0 else plane + 1) * 64
        return se[q : q + 64, :]

    def po(plane):
        if 0 <= plane < NX:
            return soo[plane * 80 : plane * 80 + 80, :]
        q = (plane + 16 if plane < 0 else plane) * 80
        return so[q : q + 80, :]

    b = pe(-17)
    for k in range(-16, 0):
        b = b + pe(k)
    t = None
    for j in range(1, 9):
        term = float(j) * (pe(-9 + j) - pe(-9 - j))
        t = term if t is None else t + term
    s2[0:64, :] = t
    for m in range(-9, 24):
        new, old = pe(m + 9), pe(m - 8)
        t = t + (8.0 * (new + old) + (old - b))
        s2[(m + 10) * 64 : (m + 11) * 64, :] = t
        if m < 23:
            b = b + (new - old)
            s1[(m + 9) * 64 : (m + 10) * 64, :] = b
    e = s1[0:64, :]
    for m in range(1, 17):
        e = e + s1[m * 64 : m * 64 + 64, :]
    xe[0:64, :] = e
    for k in range(15):
        e = e + (s1[(k + 17) * 64 : (k + 18) * 64, :] - s1[k * 64 : k * 64 + 64, :])
        xe[(k + 1) * 64 : (k + 2) * 64, :] = e
    o = s2[0:64, :]
    for m in range(1, 17):
        o = o + s2[m * 64 : m * 64 + 64, :]
    for j in range(17):
        nxt = o + (s2[(j + 17) * 64 : (j + 18) * 64, :] - s2[j * 64 : j * 64 + 64, :])
        xo[j * 64 : j * 64 + 64, :] = o + nxt
        o = nxt
    b = po(-16)
    for k in range(-15, 1):
        b = b + po(k)
    s1[0:80, :] = b
    for m in range(-8, 23):
        b = b + (po(m + 9) - po(m - 8))
        s1[(m + 9) * 80 : (m + 10) * 80, :] = b
    e = s1[0:80, :]
    for m in range(1, 17):
        e = e + s1[m * 80 : m * 80 + 80, :]
    xy[0:80, :] = e
    for k in range(15):
        e = e + (s1[(k + 17) * 80 : (k + 18) * 80, :] - s1[k * 80 : k * 80 + 80, :])
        xy[(k + 1) * 80 : (k + 2) * 80, :] = e

    mze, mzo, mzot = ze[...], zo[...], zot[...]
    for r in range(0, 1088, 64):
        xo[r : r + 64, :] = dot_rows(xo[r : r + 64, :], mze)
    for r in range(0, 1280, 80):
        xy[r : r + 80, :] = dot_rows(xy[r : r + 80, :], mze)
    for r in range(0, 1024, 64):
        xe[r : r + 64, :] = dot_rows(xe[r : r + 64, :], mzo)

    for p in range(2):
        prev = None
        for j in range(17):
            f = SCALE * xo[j * 64 + p * 32 : j * 64 + p * 32 + 32, :]
            dl, du = x_face_cells(edges, d, p, j, 0)
            cl, cu = x_face_cells(edges, c, p, j, 64)
            vb = face_bar(f, dl, du, cl, cu, {0: left, 16: right}.get(j))
            if j:
                r = (j - 1) * 64 + p * 32
                wx[r : r + 32, :] = vb + prev
            prev = vb

    for p in range(2):
        q = p * 16
        dy[pl.ds(p * 48 + 7, 16, stride=96), :] = yl[pl.ds(p * 256 + 15, 16, stride=16), :]
        dy[pl.ds(p * 48 + 40, 16, stride=96), :] = yr[pl.ds(p * 256, 16, stride=16), :]
        cy[pl.ds(p * 48 + 7, 16, stride=96), :] = yl[544 + q : 560 + q, :]
        cy[pl.ds(p * 48 + 40, 16, stride=96), :] = yr[544 + q : 560 + q, :]
        for x in range(NX):
            s = p * 512 + x * 32
            t = (x * 2 + p) * 48 + 8
            dy[t : t + 32, :] = d[s : s + 32, :]
            cy[t : t + 32, :] = c[s : s + 32, :]
    valid_y, valid_z = y_mask(), z_mask()
    for x in range(NX):
        for p in range(2):
            n = x * 2 + p
            t = n * 48
            f = (0.5 * SCALE) * xy[n * 40 : n * 40 + 40, :]
            vby[n * 40 : n * 40 + 40, :] = face_bar(
                f,
                dy[t + 7 : t + 47, :],
                dy[t + 8 : t + 48, :],
                cy[t + 7 : t + 47, :],
                cy[t + 8 : t + 48, :],
                valid_y,
            )
            s = p * 512 + x * 32
            f = (0.5 * SCALE) * xe[n * 32 : n * 32 + 32, :]
            dl, cl = d[s : s + 32, :], c[s : s + 32, :]
            du, cu = pltpu.roll(dl, NZ - 1, 1), pltpu.roll(cl, NZ - 1, 1)
            wz[n * 32 : n * 32 + 32, :] = face_bar(f, dl, du, cl, cu, valid_z)
    for n in range(32):
        wy[n * 32 : n * 32 + 32, :] = vby[n * 40 : n * 40 + 32, :] + vby[n * 40 + 1 : n * 40 + 33, :]

    for r in range(0, 1024, 64):
        wx[r : r + 64, :] = dot_rows(wx[r : r + 64, :], mze)
        wy[r : r + 64, :] = dot_rows(wy[r : r + 64, :], mze)
        wz[r : r + 64, :] = dot_rows(wz[r : r + 64, :], mzot)

    zero = jnp.zeros((64, 128), f32)

    def at(ref, plane):
        if 0 <= plane < NX:
            return ref[plane * 64 : plane * 64 + 64, :]
        return zero

    bx, t, bz, by = zero, zero, zero, zero
    for m in range(-9, 23):
        new, old = at(wx, m + 9), at(wx, m - 8)
        t = t + (8.0 * (new + old) + (old - bx))
        bx = bx + (new - old)
        bz = bz + (at(wz, m + 9) - at(wz, m - 8))
        by = by + (at(wy, m + 9) - at(wy, m - 8))
        q = (m + 9) * 64
        s1[q : q + 64, :] = bz - 2.0 * t
        s2[q : q + 64, :] = by

    def at2(ref, i):
        if 0 <= i < 32:
            return ref[i * 64 : i * 64 + 64, :]
        return zero

    matt = myt[...]
    ge, go = zero, zero
    for k in range(48):
        ge = ge + (at2(s1, k) - at2(s1, k - 17))
        go = go + (at2(s2, k) - at2(s2, k - 17))
        both = jnp.concatenate(
            [jnp.concatenate([ge[r : r + 32], go[r : r + 32]], 0) for r in (0, 32)], 1
        )
        hi, lo = split(both)
        out = dot(matt, jnp.concatenate([hi, lo], 0))
        for p in range(2):
            z = slice(p * 128, p * 128 + 128)
            if 16 <= k < 32:
                n = (k - 16) * 2 + p
                low[n * 16 : n * 16 + 16, :] = out[0:16, z]
                own[n * 32 : n * 32 + 32, :] = out[16:48, z]
                high[n * 16 : n * 16 + 16, :] = out[48:64, z]
            else:
                n = (k if k < 16 else k - 16) * 2 + p
                hm[n * 32 : n * 32 + 16, :] = out[0:16, z]
                gm[n * 32 : n * 32 + 32, :] = out[16:48, z]
                hm[n * 32 + 16 : n * 32 + 32, :] = out[48:64, z]
    to_a = pl.ds(pl.multiple_of((1 - odd_core) * 1024, 1024), 1024)
    to_b = pl.ds(pl.multiple_of(odd_core * 1024, 1024), 1024)
    am[0:1024, :] = hm[to_a, :]
    am[1024:2048, :] = gm[to_a, :]
    hb[...] = hm[to_b, :]
    gb[...] = gm[to_b, :]


def base_kernel(d, c, xo, xe, xy, cy, edges, base, tly):
    left, right = masks("gx")
    for p in range(2):
        prev = None
        for j in range(17):
            f = SCALE * xo[j * 64 + p * 32 : j * 64 + p * 32 + 32, :]
            cl, cu = x_face_cells(edges, c, p, j, 64)
            lower, upper = face_sides(f, cl, cu, {0: left, 16: right}.get(j))
            if j:
                s = p * 512 + (j - 1) * 32
                base[s : s + 32, :] = cl + (lower + prev)
            prev = upper
    valid_y, valid_z = y_mask(), z_mask()
    for x in range(NX):
        for p in range(2):
            n = x * 2 + p
            t = n * 48
            f = (0.5 * SCALE) * xy[n * 40 : n * 40 + 40, :]
            lower, upper = face_sides(f, cy[t + 7 : t + 47, :], cy[t + 8 : t + 48, :], valid_y)
            tly[n * 40 : n * 40 + 40, :] = lower
            s = p * 512 + x * 32
            f = (0.5 * SCALE) * xe[n * 32 : n * 32 + 32, :]
            cl = c[s : s + 32, :]
            lower_z, upper_z = face_sides(f, cl, pltpu.roll(cl, NZ - 1, 1), valid_z)
            base[s : s + 32, :] = (
                base[s : s + 32, :] + upper[0:32, :] + (lower_z + pltpu.roll(upper_z, 1, 1))
            )
    for x in range(NX):
        for p in range(2):
            n = x * 2 + p
            s = p * 512 + x * 32
            base[s : s + 32, :] = base[s : s + 32, :] + tly[n * 40 + 1 : n * 40 + 33, :]


def margin_kernel(low, high, ha, hb, dn, up):
    for n in range(32):
        r, q = n * 16, n * 32
        dn[r : r + 16, :] = low[r : r + 16, :] + (ha[q : q + 16, :] + hb[q : q + 16, :])
        up[r : r + 16, :] = high[r : r + 16, :] + (ha[q + 16 : q + 32, :] + hb[q + 16 : q + 32, :])


def final_kernel(av, base, own, ga, gb, yl, yr, out):
    h = 0.5 * SCALE
    weights = [h * a for a in adhesion_rows(av)]
    for x in range(NX):
        pb = []
        for p in range(2):
            q = x * 32 + p * 16
            r = 2 * q
            got = jnp.concatenate([yl[q : q + 16, :], yr[q : q + 16, :]], 0)
            pb.append(own[r : r + 32, :] + (ga[1024 + r : 1056 + r, :] + gb[r : r + 32, :]) + got)
        for p in range(2):
            s = p * 512 + x * 32
            out[s : s + 32, :] = base[s : s + 32, :] + (
                weights[p] * pb[0] + weights[2 + p] * pb[1]
            )


def rows(n):
    return jax.ShapeDtypeStruct((n, 128), f32)


def scratch(n):
    return pltpu.VMEM((n, 128), f32)


def call(kernel, args, out_rows, scratch_rows=()):
    spec = pl.BlockSpec(memory_space=pltpu.VMEM)
    total = sum(a.shape[0] for a in args) + sum(out_rows) + sum(scratch_rows)
    single = len(out_rows) == 1
    shapes = [rows(n) for n in out_rows]
    return pl.pallas_call(
        kernel,
        out_shape=shapes[0] if single else shapes,
        in_specs=[spec] * len(args),
        out_specs=spec if single else [spec] * len(out_rows),
        scratch_shapes=[scratch(n) for n in scratch_rows],
        compiler_params=pltpu.CompilerParams(vmem_limit_bytes=total * 512 + (2 << 20)),
    )(*args)


def pack(d, c):
    spec = pl.BlockSpec(memory_space=pltpu.VMEM)
    return pl.pallas_call(
        pack_kernel,
        out_shape=[rows(YROWS), rows(YROWS), rows(1024), rows(1024)],
        in_specs=[pl.BlockSpec(memory_space=pltpu.HBM)] * 2,
        out_specs=[spec] * 4,
        scratch_shapes=[pltpu.SemaphoreType.DMA((8,))],
        compiler_params=pltpu.CompilerParams(vmem_limit_bytes=54_600_000),
    )(d, c)


def spread(adhesion):
    return pl.pallas_call(
        spread_kernel,
        out_shape=rows(32),
        in_specs=[pl.BlockSpec(memory_space=pltpu.SMEM)],
        out_specs=pl.BlockSpec(memory_space=pltpu.VMEM),
        compiler_params=pltpu.CompilerParams(vmem_limit_bytes=1 << 20),
    )(adhesion)


def shift(values, axis, by):
    n = lax.axis_size(axis)
    pairs = [(i, i + by) for i in range(n) if 0 <= i + by < n]
    return lax.ppermute(values, axis, pairs)


def swap(values, first):
    n = lax.axis_size("gx")
    pairs = []
    for i in range(first, n - 1, 2):
        pairs += [(i, i + 1), (i + 1, i)]
    return lax.ppermute(values, "gx", pairs)


def step(density, cotangent, adhesion):
    my = jnp.asarray(y_matrix(), bf16)
    myt = jnp.asarray(y_transposed(), bf16)
    ze, zo, zot = (jnp.asarray(m, bf16) for m in z_matrices())
    up, dn, d, c = pack(density.reshape(1024, 128), cotangent.reshape(1024, 128))
    yl = shift(up, "gy", 1)
    yr = shift(dn, "gy", -1)
    bb = swap(d, 1)
    ba = swap(d, 0)
    av = spread(adhesion)
    ma, mb, e0, e15 = call(
        corner_kernel, [av, d, c, yl, yr], [CROWS, CROWS, 128, 128]
    )
    kb = swap(mb, 1)
    ka = swap(ma, 0)
    r2l = shift(e15, "gx", 2)
    r2r = shift(e0, "gx", -2)
    seo, soo = call(y_own_kernel, [av, d, yl, yr, my], [1024, 1280], [512])
    own, low, high, am, gb, hb, xo, xe, xy, cy, edges = call(
        main_kernel,
        [av, d, c, yl, yr, ba, bb, ka, kb, r2l, r2r, seo, soo, my, ze, zo, zot, myt],
        [1024, 512, 512, 2048, 1024, 1024, 17 * 64, 1024, 1280, 1536, 256],
        [1536, 34 * 64, 32 * 80, 32 * 80, 34 * 64, 1280, 1024, 1024, 1024, 512, 2048, 2048],
    )
    hb2 = swap(hb, 1)
    gb2 = swap(gb, 1)
    am2 = swap(am, 0)
    dn2, up2 = call(margin_kernel, [low, high, am2, hb2], [512, 512])
    yl2 = shift(up2, "gy", 1)
    yr2 = shift(dn2, "gy", -1)
    base = call(base_kernel, [d, c, xo, xe, xy, cy, edges], [1024], [1280])
    out = call(final_kernel, [av, base, own, am2, gb2, yl2, yr2], [1024])
    return out.reshape(density.shape)


def solution(mesh):
    return jax.shard_map(
        step,
        mesh=mesh,
        in_specs=(P(None, "gx", "gy", None), P(None, "gx", "gy", None), P()),
        out_specs=P(None, "gx", "gy", None),
        check_vma=False,
    )
```
